32 devices in a mesh: cells: 4 (over x, core), modes: 8 (over z, y).
Axes of the slice: x: 2, y: 2, z: 4, core: 2. Of those that a mesh axis runs over, the one named last changes fastest.
Arguments:
- hermite_coefficient_array: float32 [8, 64, 32, 2048], P('cells', None, None, 'modes'), may hold values from -6 to 6
- encounter_kernel_array: bfloat16 [14400, 120], replicated, may hold values from -0.046875 to 0.046875
- obstacle_indicator: int32 [8, 64, 32], P('cells'), may hold values 0 or 1
Outputs:
- moments_next: float32 [8, 64, 32, 2048], P('cells', None, None, 'modes')
The draws below stay inside these ranges and needn't reach their ends.
All inputs are finite; a program needn't handle non-finite values. No bound on the sum of `obstacle_indicator` on one device may be relied on, other than what follows from the above.
Results may differ from the reference program's by a relative error of at most 0.0003.
Values sent between devices are 32-bit elements; how exact they have to be, the bound alone decides.
A program may use at most 128 MiB of HBM per device.

```python
import math
import jax
import jax.numpy as jnp
from jax import lax

NY = 64
NZ = 32
MA = 16
MB = 16
MC = 8
LDEG = 7
BASIS_SIZE = 120
MODES = 2048
NX = 8


def plant(array, own_key, smallest, largest):
    extent = array.shape
    index_at = [jax.random.randint(jax.random.fold_in(own_key, axis), (), 0, extent[axis]) for axis in range(len(extent))]
    array = array.at[tuple(index_at)].set(smallest)
    longest = extent.index(max(extent))
    index_at[longest] = (index_at[longest] + 1) % extent[longest]
    return array.at[tuple(index_at)].set(largest)


def block_levels(own_key, dims, shards, least, high):
    level, own = 1.0, jax.random.fold_in(own_key, 6)
    for position, parts in shards:
        heights = jnp.exp(jax.random.uniform(jax.random.fold_in(own, position), (parts,), jnp.float32, least / len(shards), high / len(shards)))
        level = level * jnp.repeat(heights, dims[position] // parts).reshape([-1 if axis == position else 1 for axis in range(len(dims))])
    return level


def normal_values(key, shape, deviation, limit, shards=(), held_as=jnp.bfloat16):
    entries = deviation * jax.random.normal(key, shape, jnp.float32)
    if shards:
        entries = entries * block_levels(key, shape, shards, -0.22, 0.18)
    return jnp.clip(entries, -limit, limit).astype(held_as)


def setup_inputs(seed: int = 0) -> dict:
    key_list = jax.random.split(jax.random.key(seed), 4)
    return {
        "hermite_coefficient_array": normal_values(key_list[0], (NX, NY, NZ, MODES), 1.0, 6.0, ((0, 4), (3, 8)), jnp.float32),
        "encounter_kernel_array": normal_values(key_list[1], (BASIS_SIZE * BASIS_SIZE, BASIS_SIZE), (BASIS_SIZE * BASIS_SIZE) ** -0.5, 0.046875),
        "obstacle_indicator": plant((jax.random.randint(key_list[2], (NX, NY, NZ), 0, 8) < 1).astype(jnp.int32), jax.random.fold_in(key_list[2], 1), 0, 1),
    }


CFL = 0.04
DTC = 0.2

def ladder_ref(field, axis):
    count = field.shape[axis]
    pad_spec = [(0, 0)] * field.ndim
    pad_spec[axis] = (1, 1)
    padded = jnp.pad(field, pad_spec)
    lower_part = lax.slice_in_dim(padded, 0, count, axis=axis)
    upper_part = lax.slice_in_dim(padded, 2, count + 2, axis=axis)
    shape_list = [1] * field.ndim
    shape_list[axis] = count
    level = jnp.arange(count, dtype=jnp.float32).reshape(shape_list)
    return jnp.sqrt(level) * lower_part + jnp.sqrt(level + 1.0) * upper_part

def transport(grid, obstacle_indicator):
    speed_x = 2.0 * math.sqrt(MA)
    speed_y = 2.0 * math.sqrt(MB)
    speed_z = 2.0 * math.sqrt(MC)

    def plane(plane_index):
        center = lax.dynamic_index_in_dim(grid, plane_index, 0, keepdims=False)
        behind = lax.dynamic_index_in_dim(grid, jnp.mod(plane_index - 1, NX), 0, keepdims=False)
        beyond = lax.dynamic_index_in_dim(grid, jnp.mod(plane_index + 1, NX), 0, keepdims=False)
        solid = lax.dynamic_index_in_dim(obstacle_indicator, plane_index, 0, keepdims=False)
        first_axis_gradient = beyond - behind
        lap_x = beyond - 2.0 * center + behind
        next_y = jnp.roll(center, -1, 0)
        prev_y = jnp.roll(center, 1, 0)
        next_z = jnp.roll(center, -1, 1)
        prev_z = jnp.roll(center, 1, 1)
        diff_y = next_y - prev_y
        lap_y = next_y - 2.0 * center + prev_y
        diff_z = next_z - prev_z
        lap_z = next_z - 2.0 * center + prev_z
        shaped = (NY, NZ, MA, MB, MC)
        flux = ladder_ref(first_axis_gradient.reshape(shaped), 2) + ladder_ref(diff_y.reshape(shaped), 3) + ladder_ref(diff_z.reshape(shaped), 4)
        flux = flux.reshape(NY, NZ, MODES)
        update = center + CFL * (-0.5 * flux + 0.5 * (speed_x * lap_x + speed_y * lap_y + speed_z * lap_z))
        return jnp.where(solid[..., None] != 0, center, update)
    return lax.map(plane, jnp.arange(NX, dtype=jnp.int32))

def reference(hermite_coefficient_array, encounter_kernel_array, obstacle_indicator):
    grid = hermite_coefficient_array
    for repeat in range(2):
        grid = transport(grid, obstacle_indicator)
    rows = grid.reshape(NX * NY * NZ, MODES)
    mode_index = jnp.arange(MODES, dtype=jnp.int32)
    degree = mode_index // (MB * MC) + mode_index // MC % MB + mode_index % MC
    low_index = jnp.nonzero(degree <= LDEG, size=BASIS_SIZE)[0].astype(jnp.int32)
    low = rows[:, low_index]

    def collide(block_rows):
        quadratic_factors = (block_rows[:, :, None] * block_rows[:, None, :]).reshape(block_rows.shape[0], BASIS_SIZE * BASIS_SIZE).astype(jnp.bfloat16)
        return jnp.dot(quadratic_factors, encounter_kernel_array, preferred_element_type=jnp.float32)
    scattered_state = lax.map(collide, low.reshape(-1, 512, BASIS_SIZE)).reshape(-1, BASIS_SIZE)
    rows = rows.at[:, low_index].add(DTC * scattered_state)
    return rows.reshape(NX, NY, NZ, MODES)
```

```python
import functools
import math

import jax
import jax.numpy as jnp
from jax import lax
from jax.experimental import pallas as pl
from jax.experimental.pallas import tpu as pltpu
from jax.sharding import PartitionSpec as P

MA = 16
MB = 16
MC = 8
LDEG = 7
BASIS_SIZE = 120
MODES = 2048
BLOCK = MB * MC
WIDE = 128
GROUP = 8

CFL = 0.04
DTC = 0.2
MESH = pl.DeviceIdType.MESH


def pieces_of(edges, half):
    marks = sorted(set(edges) | {2, half + 2})
    return [(lo, hi) for lo, hi in zip(marks[:-1], marks[1:])]


def split3(x):
    hi = x.astype(jnp.bfloat16)
    rest = x - hi.astype(jnp.float32)
    mid = rest.astype(jnp.bfloat16)
    low = (rest - mid.astype(jnp.float32)).astype(jnp.bfloat16)
    return hi, mid, low


def dot(a, b):
    return jnp.dot(a, b, preferred_element_type=jnp.float32)


def kernel(cfg, hin, mask, coef, sel, sel_t, kern, out, f0, f1, tr, xh1, xh2, zh1, zh2, de1, de2,
           lx, lr, rx, rr, loc_sem, swap_s, swap_r, x1_s, x1_r, x2_s, x2_r, z1_s, z1_r, z2_s, z2_r,
           low_s, low_r, rate_s, rate_r, back_s, back_r, keep_sem):
    planes, rows_y, rows_z, local, nc, nm, ns, chunks = cfg
    per = local // BLOCK
    levels = 2 * per
    half = rows_y // 2
    nq = nm // 2
    size = half // chunks
    b2 = [2 + size * k for k in range(chunks + 1)]
    b1 = [1] + [b + 1 for b in b2[1:]]
    b0 = [0] + [b + 2 for b in b2[1:]]
    part = size // ns

    c = lax.axis_index("cells")
    m = lax.axis_index("modes")
    p = lax.rem(m, 2)
    q = lax.div(m, 2)
    other = 1 - p
    mate = (c, q * 2 + other)
    before = (lax.rem(c + nc - 1, nc), m)
    after = (lax.rem(c + 1, nc), m)
    below = (c, m - 2)
    above = (c, m + 2)
    has_below = q > 0
    has_above = q < nq - 1
    is_source = q < ns

    def peer(d):
        return (c, lax.rem(q + d, ns) * 2 + p)

    barrier = pltpu.get_barrier_semaphore()

    def greet(dev):
        pl.semaphore_signal(barrier, inc=1, device_id=dev, device_id_type=MESH)

    for dev in (mate, before, after):
        greet(dev)

    @pl.when(has_below)
    def _():
        greet(below)

    @pl.when(has_above)
    def _():
        greet(above)

    @pl.when(is_source)
    def _():
        for d in range(1, ns):
            greet(peer(d))

    greeted = 3 + has_below.astype(jnp.int32) + has_above.astype(jnp.int32)
    pl.semaphore_wait(barrier, greeted + (ns - 1) * is_source.astype(jnp.int32))

    def remote(src, dst, s, r, dev):
        return pltpu.make_async_remote_copy(
            src_ref=src, dst_ref=dst, send_sem=s, recv_sem=r, device_id=dev, device_id_type=MESH
        )

    pieces = pieces_of(b0, half)

    def grid_row(side, e):
        return lax.rem(side * half + (rows_y - 2) + e, rows_y)

    def swap(i):
        lo, hi = pieces[i]
        return remote(
            hin.at[:, pl.ds(grid_row(other, lo), hi - lo)],
            f0.at[p, :, pl.ds(lo, hi - lo)],
            swap_s.at[i], swap_r.at[i], mate,
        )

    def swap_in(i):
        lo, hi = pieces[i]
        return remote(
            hin.at[:, pl.ds(grid_row(other, lo), hi - lo)],
            f0.at[other, :, pl.ds(lo, hi - lo)],
            swap_s.at[i], swap_r.at[i], mate,
        )

    def own(i):
        lo, hi = pieces[i]
        return pltpu.make_async_copy(
            hin.at[:, pl.ds(grid_row(p, lo), hi - lo)],
            f0.at[p, :, pl.ds(lo, hi - lo)],
            loc_sem.at[i],
        )

    def edge(field, halo, ss, rs, blk, k, slot, bounds):
        n = bounds[k + 1] - bounds[k]
        where = pl.ds(bounds[k], n)
        up = remote(field.at[blk, planes - 1, where], halo.at[0, blk, where],
                    ss.at[0, slot, k], rs.at[0, slot, k], after)
        down = remote(field.at[blk, 0, where], halo.at[1, blk, where],
                      ss.at[1, slot, k], rs.at[1, slot, k], before)
        return up, down

    def lanes(j):
        return pl.ds((j % per) * BLOCK, BLOCK)

    def gradient(field, halo, pln, e, j):
        blk = j // per
        nxt = halo[1, blk, e, :, lanes(j)] if pln == planes - 1 else field[blk, pln + 1, e, :, lanes(j)]
        prv = halo[0, blk, e, :, lanes(j)] if pln == 0 else field[blk, pln - 1, e, :, lanes(j)]
        return nxt, prv

    def slopes(field, halo, de, lo, hi):
        def row(e, carry):
            for pln in range(planes):
                nxt, prv = gradient(field, halo, pln, e, 0)
                de[0, pln, e] = nxt - prv
                nxt, prv = gradient(field, halo, pln, e, levels - 1)
                de[1, pln, e] = nxt - prv
            return carry

        lax.fori_loop(lo, hi, row, 0)

    def to_below(de, zh, ss, rs, k, bounds):
        where = pl.ds(bounds[k], bounds[k + 1] - bounds[k])
        return remote(de.at[0, :, where], zh.at[1, :, where], ss.at[0, k], rs.at[0, k], below)

    def to_above(de, zh, ss, rs, k, bounds):
        where = pl.ds(bounds[k], bounds[k + 1] - bounds[k])
        return remote(de.at[1, :, where], zh.at[0, :, where], ss.at[1, k], rs.at[1, k], above)

    def z_start(*a):
        @pl.when(has_below)
        def _():
            to_below(*a).start()

        @pl.when(has_above)
        def _():
            to_above(*a).start()

    def z_arrived(*a):
        @pl.when(has_below)
        def _():
            to_above(*a).wait_recv()

        @pl.when(has_above)
        def _():
            to_below(*a).wait_recv()

    def z_sent(*a):
        @pl.when(has_below)
        def _():
            to_below(*a).wait_send()

        @pl.when(has_above)
        def _():
            to_above(*a).wait_send()

    wx = 0.5 * 2.0 * math.sqrt(MA)
    wy = 0.5 * 2.0 * math.sqrt(MB)
    wz = 0.5 * 2.0 * math.sqrt(MC)
    wc = 2.0 * (wx + wy + wz)

    def substep(field, halo, zh, dest, lo, hi):
        def row(e, carry):
            for pln in range(planes):
                gas = mask[pln, e]
                pairs = [gradient(field, halo, pln, e, j) for j in range(levels)]
                grads = [zh[0, pln, e]] + [a - b for a, b in pairs] + [zh[1, pln, e]]
                for j in range(levels):
                    blk = j // per
                    mid = field[blk, pln, e, :, lanes(j)]
                    ny = field[blk, pln, e + 1, :, lanes(j)]
                    py = field[blk, pln, e - 1, :, lanes(j)]
                    nz = pltpu.roll(mid, rows_z - 1, 0)
                    pz = pltpu.roll(mid, 1, 0)
                    dy = ny - py
                    dz = nz - pz
                    acc = coef[4 + j : 5 + j, :] * grads[j]
                    acc += coef[4 + levels + j : 5 + levels + j, :] * grads[j + 2]
                    acc += coef[0:1, :] * pltpu.roll(dy, MC, 1)
                    acc += coef[1:2, :] * pltpu.roll(dy, BLOCK - MC, 1)
                    acc += coef[2:3, :] * pltpu.roll(dz, 1, 1)
                    acc += coef[3:4, :] * pltpu.roll(dz, BLOCK - 1, 1)
                    acc += wx * (pairs[j][0] + pairs[j][1]) + wy * (ny + py) + wz * (nz + pz) - wc * mid
                    dest[blk, pln, e, :, lanes(j)] = mid + gas * acc
            return carry

        lax.fori_loop(lo, hi, row, 0)

    def take_low(k):
        for t in range(ns):
            lo = b2[k] + t * part
            for pln in range(planes):
                total = jnp.zeros((part * rows_z, WIDE), jnp.float32)
                for j in range(levels):
                    x = tr[j // per, pln, lo : lo + part, :, lanes(j)].reshape(part * rows_z, BLOCK)
                    for term in split3(x):
                        total += dot(term, sel[j])
                lx[k, t, pln * part * rows_z : (pln + 1) * part * rows_z] = total

    def low_copy(k, d):
        return remote(lx.at[k, lax.rem(q + d, ns)], lr.at[k, d - 1],
                      low_s.at[k, d - 1], low_r.at[k, d - 1], peer(d))

    def rate_copy(k, d):
        return remote(rx.at[k], rr.at[k, d - 1], rate_s.at[k, d - 1], rate_r.at[k, d - 1], peer(d))

    def collide(k):
        low = lx[k, q]
        for d in range(1, ns):
            low = low + lr[k, d - 1]
        lx[k, q] = low
        rx[k] = jnp.zeros_like(low)

        def step(g, carry):
            values = lx[k, q]
            turned = pltpu.roll(values, lax.rem(WIDE - g * GROUP, WIDE), 1)
            factors = jnp.concatenate(
                [(turned[:, i : i + 1] * values).astype(jnp.bfloat16) for i in range(GROUP)], axis=1
            )
            first = pl.multiple_of(g * (GROUP * WIDE), GROUP * WIDE)
            rx[k] += dot(factors, kern[pl.ds(first, GROUP * WIDE), :])
            return carry

        lax.fori_loop(0, BASIS_SIZE // GROUP, step, 0)

    def lift(k, rates, t):
        lo = b2[k] + t * part
        terms = split3(rates)
        for j in range(levels):
            add = sum(dot(term, sel_t[j]) for term in terms) * DTC
            for pln in range(planes):
                one = add[pln * part * rows_z : (pln + 1) * part * rows_z]
                tr[j // per, pln, pl.ds(lo, part), :, lanes(j)] += one.reshape(part, rows_z, BLOCK)

    def give_back(k):
        return remote(
            tr.at[other, :, pl.ds(b2[k], size)],
            out.at[:, pl.ds(p * half + k * size, size)],
            back_s.at[k], back_r.at[k], mate,
        )

    def got_back(k):
        return remote(
            tr.at[other, :, pl.ds(b2[k], size)],
            out.at[:, pl.ds(other * half + k * size, size)],
            back_s.at[k], back_r.at[k], mate,
        )

    def keep(k):
        return pltpu.make_async_copy(
            tr.at[p, :, pl.ds(b2[k], size)],
            out.at[:, pl.ds(p * half + k * size, size)],
            keep_sem.at[k],
        )

    def finish(k):
        give_back(k).start()
        keep(k).start()

    for i in range(len(pieces)):
        swap(i).start()
    for i in range(len(pieces)):
        own(i).start()

    @pl.when(q == 0)
    def _():
        for zh in (zh1, zh2):
            zh[0] = jnp.zeros_like(zh[0])

    @pl.when(q == nq - 1)
    def _():
        for zh in (zh1, zh2):
            zh[1] = jnp.zeros_like(zh[1])

    for i in range(len(pieces)):
        own(i).wait()
    for k in range(chunks):
        for copy in edge(f0, xh1, x1_s, x1_r, p, k, 0, b1):
            copy.start()

    done = 0
    for k in range(chunks + 2):
        if k < chunks:
            while done < len(pieces) and pieces[done][1] <= b0[k + 1]:
                swap_in(done).wait_recv()
                done += 1
            for copy in edge(f0, xh1, x1_s, x1_r, other, k, 1, b1):
                copy.start()
        if 0 <= k - 1 < chunks:
            i = k - 1
            for copy in edge(f0, xh1, x1_s, x1_r, p, i, 0, b1):
                copy.wait_recv()
            for copy in edge(f0, xh1, x1_s, x1_r, other, i, 1, b1):
                copy.wait_recv()
            slopes(f0, xh1, de1, b1[i], b1[i + 1])
            z_start(de1, zh1, z1_s, z1_r, i, b1)
        if 0 <= k - 2 < chunks:
            i = k - 2
            z_arrived(de1, zh1, z1_s, z1_r, i, b1)
            substep(f0, xh1, zh1, f1, b1[i], b1[i + 1])
            for blk in range(2):
                for copy in edge(f1, xh2, x2_s, x2_r, blk, i, blk, b2):
                    copy.start()

    for k in range(chunks + 3):
        if k < chunks:
            for blk in range(2):
                for copy in edge(f1, xh2, x2_s, x2_r, blk, k, blk, b2):
                    copy.wait_recv()
            slopes(f1, xh2, de2, b2[k], b2[k + 1])
            z_start(de2, zh2, z2_s, z2_r, k, b2)
        if 0 <= k - 1 < chunks:
            i = k - 1
            z_arrived(de2, zh2, z2_s, z2_r, i, b2)
            substep(f1, xh2, zh2, tr, b2[i], b2[i + 1])

            @pl.when(is_source)
            def _(i=i):
                take_low(i)
                for d in range(1, ns):
                    low_copy(i, d).start()

            @pl.when(jnp.logical_not(is_source))
            def _(i=i):
                finish(i)

        @pl.when(is_source)
        def _(k=k):
            if 0 <= k - 2 < chunks:
                i = k - 2
                for d in range(1, ns):
                    low_copy(i, d).wait_recv()
                collide(i)
                for d in range(1, ns):
                    rate_copy(i, d).start()
                lift(i, rx[i], q)
            if 0 <= k - 3 < chunks:
                i = k - 3
                for d in range(1, ns):
                    rate_copy(i, d).wait_recv()
                    lift(i, rr[i, d - 1], lax.rem(q + ns - d, ns))
                finish(i)

    for k in range(chunks):
        z_sent(de1, zh1, z1_s, z1_r, k, b1)
        z_sent(de2, zh2, z2_s, z2_r, k, b2)
        for slot, blk in enumerate((p, other)):
            for copy in edge(f0, xh1, x1_s, x1_r, blk, k, slot, b1):
                copy.wait_send()
        for blk in range(2):
            for copy in edge(f1, xh2, x2_s, x2_r, blk, k, blk, b2):
                copy.wait_send()
    for i in range(len(pieces)):
        swap(i).wait_send()

    @pl.when(is_source)
    def _():
        for k in range(chunks):
            for d in range(1, ns):
                low_copy(k, d).wait_send()
                rate_copy(k, d).wait_send()

    for k in range(chunks):
        keep(k).wait()
        give_back(k).wait_send()
        got_back(k).wait_recv()


def body(hermite_coefficient_array, encounter_kernel_array, obstacle_indicator):
    planes, rows_y, rows_z, local = hermite_coefficient_array.shape
    nc = lax.axis_size("cells")
    nm = lax.axis_size("modes")
    per = local // BLOCK
    levels = 2 * per
    half = rows_y // 2
    ns = -(-(LDEG + 1) // levels)
    chunks = 4
    size = half // chunks
    part = size // ns
    ext = half + 4
    m = lax.axis_index("modes")
    first_a = (m // 2) * levels

    gas = jnp.where(obstacle_indicator != 0, 0.0, CFL).astype(jnp.float32)
    gas = jnp.concatenate([gas[:, -2:], gas, gas[:, :2]], axis=1)
    gas = lax.dynamic_slice_in_dim(gas, (m % 2) * half, ext, axis=1)
    mask = jnp.broadcast_to(gas[..., None], (planes, ext, rows_z, BLOCK))

    lane = jnp.arange(BLOCK, dtype=jnp.int32)
    lane_b, lane_c = lane // MC, lane % MC
    level = first_a + jnp.arange(levels, dtype=jnp.int32)[:, None] + 0 * lane[None, :]

    def down(x):
        return jnp.sqrt(x.astype(jnp.float32))

    def up(x, count):
        return jnp.where(x + 1 < count, jnp.sqrt((x + 1).astype(jnp.float32)), 0.0)

    coef = -0.5 * jnp.concatenate(
        [
            jnp.stack([down(lane_b), up(lane_b, MB), down(lane_c), up(lane_c, MC)]),
            down(level),
            up(level, MA),
            jnp.zeros(((-(4 + 2 * levels)) % 8, BLOCK), jnp.float32),
        ],
        axis=0,
    )

    index = jnp.arange(MODES, dtype=jnp.int32)
    flags = (index // BLOCK + index // MC % MB + index % MC <= LDEG).astype(jnp.int32)
    rank = jnp.where(flags == 1, jnp.cumsum(flags) - 1, -1)
    mine = lax.dynamic_slice_in_dim(rank, first_a * BLOCK, levels * BLOCK).reshape(levels, BLOCK)
    wide = jnp.arange(WIDE, dtype=jnp.int32)
    sel = (mine[:, :, None] == wide[None, None, :]).astype(jnp.bfloat16)
    sel_t = (mine[:, None, :] == wide[None, :, None]).astype(jnp.bfloat16)

    kern = encounter_kernel_array.reshape(BASIS_SIZE, BASIS_SIZE, BASIS_SIZE)
    kern = jnp.pad(kern, ((0, 0), (0, WIDE - BASIS_SIZE), (0, WIDE - BASIS_SIZE)))
    kern = kern.reshape(BASIS_SIZE * WIDE, WIDE)

    b2 = [2 + size * k for k in range(chunks + 1)]
    count = len(pieces_of([0] + [b + 2 for b in b2[1:]], half))
    peers = max(ns - 1, 1)
    cells = planes * part * rows_z
    field = pltpu.VMEM((2, planes, ext, rows_z, local), jnp.float32)
    halo = pltpu.VMEM((2, 2, ext, rows_z, local), jnp.float32)
    slope = pltpu.VMEM((2, planes, ext, rows_z, BLOCK), jnp.float32)
    dma = pltpu.SemaphoreType.DMA
    cfg = (planes, rows_y, rows_z, local, nc, nm, ns, chunks)
    vmem = pl.BlockSpec(memory_space=pltpu.VMEM)
    return pl.pallas_call(
        functools.partial(kernel, cfg),
        out_shape=jax.ShapeDtypeStruct(hermite_coefficient_array.shape, jnp.float32),
        in_specs=[pl.BlockSpec(memory_space=pl.ANY)] + [vmem] * 5,
        out_specs=pl.BlockSpec(memory_space=pl.ANY),
        scratch_shapes=[
            field, field, field, halo, halo, slope, slope, slope, slope,
            pltpu.VMEM((chunks, ns, cells, WIDE), jnp.float32),
            pltpu.VMEM((chunks, peers, cells, WIDE), jnp.float32),
            pltpu.VMEM((chunks, cells, WIDE), jnp.float32),
            pltpu.VMEM((chunks, peers, cells, WIDE), jnp.float32),
            dma((count,)), dma((count,)), dma((count,)),
            dma((2, 2, chunks)), dma((2, 2, chunks)), dma((2, 2, chunks)), dma((2, 2, chunks)),
            dma((2, chunks)), dma((2, chunks)), dma((2, chunks)), dma((2, chunks)),
            dma((chunks, peers)), dma((chunks, peers)), dma((chunks, peers)), dma((chunks, peers)),
            dma((chunks,)), dma((chunks,)), dma((chunks,)),
        ],
        compiler_params=pltpu.CompilerParams(
            collective_id=0, has_side_effects=True, vmem_limit_bytes=60 * 1024 * 1024
        ),
    )(hermite_coefficient_array, mask, coef, sel, sel_t, kern)


def solution(mesh):
    placed = (P("cells", None, None, "modes"), P(), P("cells", None, None))
    return jax.shard_map(
        body, mesh=mesh, in_specs=placed, out_specs=P("cells", None, None, "modes"), check_vma=False
    )
```

```python
import functools
import math

import jax
import jax.numpy as jnp
import numpy as np
from jax import lax
from jax.experimental import pallas as pl
from jax.experimental.pallas import tpu as pltpu
from jax.sharding import PartitionSpec as P

MA = 16
MB = 16
MC = 8
LDEG = 7
BASIS_SIZE = 120
MODES = 2048
BLOCK = MB * MC
WIDE = 128
GROUP = 8

CFL = 0.04
DTC = 0.2
MESH = pl.DeviceIdType.MESH


def pieces_of(edges, half):
    marks = sorted(set(edges) | {2, half + 2})
    return [(lo, hi) for lo, hi in zip(marks[:-1], marks[1:])]


def split3(x):
    hi = x.astype(jnp.bfloat16)
    rest = x - hi.astype(jnp.float32)
    mid = rest.astype(jnp.bfloat16)
    low = (rest - mid.astype(jnp.float32)).astype(jnp.bfloat16)
    return hi, mid, low


def dot(a, b):
    return jnp.dot(a, b, preferred_element_type=jnp.float32)


def kernel(cfg, hin, mask, coef, sel, sel_t, raw, out, f0, f1, tr, xh1, xh2, zh1, zh2, de1, de2,
           lx, lr, rx, rr, plain, kern, raw_sem, loc_sem, swap_s, swap_r, x1_s, x1_r, x2_s, x2_r, z1_s, z1_r, z2_s, z2_r,
           low_s, low_r, rate_s, rate_r, back_s, back_r, keep_sem):
    planes, rows_y, rows_z, local, nc, nm, ns, chunks = cfg
    per = local // BLOCK
    levels = 2 * per
    half = rows_y // 2
    nq = nm // 2
    size = half // chunks
    b2 = [2 + size * k for k in range(chunks + 1)]
    b1 = [1] + [b + 1 for b in b2[1:]]
    b0 = [0] + [b + 2 for b in b2[1:]]
    part = size // ns

    c = lax.axis_index("cells")
    m = lax.axis_index("modes")
    p = lax.rem(m, 2)
    q = lax.div(m, 2)
    other = 1 - p
    mate = (c, q * 2 + other)
    before = (lax.rem(c + nc - 1, nc), m)
    after = (lax.rem(c + 1, nc), m)
    below = (c, m - 2)
    above = (c, m + 2)
    has_below = q > 0
    has_above = q < nq - 1
    is_source = q < ns

    def peer(d):
        return (c, lax.rem(q + d, ns) * 2 + p)

    barrier = pltpu.get_barrier_semaphore()

    def greet(dev):
        pl.semaphore_signal(barrier, inc=1, device_id=dev, device_id_type=MESH)

    for dev in (mate, before, after):
        greet(dev)

    @pl.when(has_below)
    def _():
        greet(below)

    @pl.when(has_above)
    def _():
        greet(above)

    @pl.when(is_source)
    def _():
        for d in range(1, ns):
            greet(peer(d))

    greeted = 3 + has_below.astype(jnp.int32) + has_above.astype(jnp.int32)
    pl.semaphore_wait(barrier, greeted + (ns - 1) * is_source.astype(jnp.int32))

    def remote(src, dst, s, r, dev):
        return pltpu.make_async_remote_copy(
            src_ref=src, dst_ref=dst, send_sem=s, recv_sem=r, device_id=dev, device_id_type=MESH
        )

    pieces = pieces_of(b0, half)

    def grid_row(side, e):
        return lax.rem(side * half + (rows_y - 2) + e, rows_y)

    def swap(i):
        lo, hi = pieces[i]
        return remote(
            hin.at[:, pl.ds(grid_row(other, lo), hi - lo)],
            f0.at[p, :, pl.ds(lo, hi - lo)],
            swap_s.at[i], swap_r.at[i], mate,
        )

    def swap_in(i):
        lo, hi = pieces[i]
        return remote(
            hin.at[:, pl.ds(grid_row(other, lo), hi - lo)],
            f0.at[other, :, pl.ds(lo, hi - lo)],
            swap_s.at[i], swap_r.at[i], mate,
        )

    def own(i):
        lo, hi = pieces[i]
        return pltpu.make_async_copy(
            hin.at[:, pl.ds(grid_row(p, lo), hi - lo)],
            f0.at[p, :, pl.ds(lo, hi - lo)],
            loc_sem.at[i],
        )

    def edge(field, halo, ss, rs, blk, k, slot, bounds):
        n = bounds[k + 1] - bounds[k]
        where = pl.ds(bounds[k], n)
        up = remote(field.at[blk, planes - 1, where], halo.at[0, blk, where],
                    ss.at[0, slot, k], rs.at[0, slot, k], after)
        down = remote(field.at[blk, 0, where], halo.at[1, blk, where],
                      ss.at[1, slot, k], rs.at[1, slot, k], before)
        return up, down

    def lanes(j):
        return pl.ds((j % per) * BLOCK, BLOCK)

    def gradient(field, halo, pln, e, j):
        blk = j // per
        nxt = halo[1, blk, e, :, lanes(j)] if pln == planes - 1 else field[blk, pln + 1, e, :, lanes(j)]
        prv = halo[0, blk, e, :, lanes(j)] if pln == 0 else field[blk, pln - 1, e, :, lanes(j)]
        return nxt, prv

    def slopes(field, halo, de, lo, hi):
        def row(e, carry):
            for pln in range(planes):
                nxt, prv = gradient(field, halo, pln, e, 0)
                de[0, pln, e] = nxt - prv
                nxt, prv = gradient(field, halo, pln, e, levels - 1)
                de[1, pln, e] = nxt - prv
            return carry

        lax.fori_loop(lo, hi, row, 0)

    def to_below(de, zh, ss, rs, k, bounds):
        where = pl.ds(bounds[k], bounds[k + 1] - bounds[k])
        return remote(de.at[0, :, where], zh.at[1, :, where], ss.at[0, k], rs.at[0, k], below)

    def to_above(de, zh, ss, rs, k, bounds):
        where = pl.ds(bounds[k], bounds[k + 1] - bounds[k])
        return remote(de.at[1, :, where], zh.at[0, :, where], ss.at[1, k], rs.at[1, k], above)

    def z_start(*a):
        @pl.when(has_below)
        def _():
            to_below(*a).start()

        @pl.when(has_above)
        def _():
            to_above(*a).start()

    def z_arrived(*a):
        @pl.when(has_below)
        def _():
            to_above(*a).wait_recv()

        @pl.when(has_above)
        def _():
            to_below(*a).wait_recv()

    def z_sent(*a):
        @pl.when(has_below)
        def _():
            to_below(*a).wait_send()

        @pl.when(has_above)
        def _():
            to_above(*a).wait_send()

    wx = 0.5 * 2.0 * math.sqrt(MA)
    wy = 0.5 * 2.0 * math.sqrt(MB)
    wz = 0.5 * 2.0 * math.sqrt(MC)
    wc = 2.0 * (wx + wy + wz)

    def substep(field, halo, zh, dest, lo, hi):
        def row(e, carry):
            for pln in range(planes):
                gas = mask[pln, e]
                pairs = [gradient(field, halo, pln, e, j) for j in range(levels)]
                grads = [zh[0, pln, e]] + [a - b for a, b in pairs] + [zh[1, pln, e]]
                for j in range(levels):
                    blk = j // per
                    mid = field[blk, pln, e, :, lanes(j)]
                    ny = field[blk, pln, e + 1, :, lanes(j)]
                    py = field[blk, pln, e - 1, :, lanes(j)]
                    nz = pltpu.roll(mid, rows_z - 1, 0)
                    pz = pltpu.roll(mid, 1, 0)
                    dy = ny - py
                    dz = nz - pz
                    acc = coef[4 + j : 5 + j, :] * grads[j]
                    acc += coef[4 + levels + j : 5 + levels + j, :] * grads[j + 2]
                    acc += coef[0:1, :] * pltpu.roll(dy, MC, 1)
                    acc += coef[1:2, :] * pltpu.roll(dy, BLOCK - MC, 1)
                    acc += coef[2:3, :] * pltpu.roll(dz, 1, 1)
                    acc += coef[3:4, :] * pltpu.roll(dz, BLOCK - 1, 1)
                    acc += wx * (pairs[j][0] + pairs[j][1]) + wy * (ny + py) + wz * (nz + pz) - wc * mid
                    dest[blk, pln, e, :, lanes(j)] = mid + gas * acc
            return carry

        lax.fori_loop(lo, hi, row, 0)

    def take_low(k):
        for t in range(ns):
            lo = b2[k] + t * part
            for pln in range(planes):
                total = jnp.zeros((part * rows_z, WIDE), jnp.float32)
                for j in range(levels):
                    x = tr[j // per, pln, lo : lo + part, :, lanes(j)].reshape(part * rows_z, BLOCK)
                    for term in split3(x):
                        total += dot(term, sel[j])
                lx[k, t, pln * part * rows_z : (pln + 1) * part * rows_z] = total

    def low_copy(k, d):
        return remote(lx.at[k, lax.rem(q + d, ns)], lr.at[k, d - 1],
                      low_s.at[k, d - 1], low_r.at[k, d - 1], peer(d))

    def rate_copy(k, d):
        return remote(rx.at[k], rr.at[k, d - 1], rate_s.at[k, d - 1], rate_r.at[k, d - 1], peer(d))

    def collide(k):
        low = lx[k, q]
        for d in range(1, ns):
            low = low + lr[k, d - 1]
        lx[k, q] = low
        rx[k] = jnp.zeros_like(low)

        def step(g, carry):
            values = lx[k, q]
            turned = pltpu.roll(values, lax.rem(WIDE - g * GROUP, WIDE), 1)
            factors = jnp.concatenate(
                [(turned[:, i : i + 1] * values).astype(jnp.bfloat16) for i in range(GROUP)], axis=1
            )
            first = pl.multiple_of(g * (GROUP * WIDE), GROUP * WIDE)
            rx[k] += dot(factors, kern[pl.ds(first, GROUP * WIDE), :])
            return carry

        lax.fori_loop(0, BASIS_SIZE // GROUP, step, 0)

    def lift(k, rates, t):
        lo = b2[k] + t * part
        terms = split3(rates)
        for j in range(levels):
            add = sum(dot(term, sel_t[j]) for term in terms) * DTC
            for pln in range(planes):
                one = add[pln * part * rows_z : (pln + 1) * part * rows_z]
                tr[j // per, pln, pl.ds(lo, part), :, lanes(j)] += one.reshape(part, rows_z, BLOCK)

    def give_back(k):
        return remote(
            tr.at[other, :, pl.ds(b2[k], size)],
            out.at[:, pl.ds(p * half + k * size, size)],
            back_s.at[k], back_r.at[k], mate,
        )

    def got_back(k):
        return remote(
            tr.at[other, :, pl.ds(b2[k], size)],
            out.at[:, pl.ds(other * half + k * size, size)],
            back_s.at[k], back_r.at[k], mate,
        )

    def keep(k):
        return pltpu.make_async_copy(
            tr.at[p, :, pl.ds(b2[k], size)],
            out.at[:, pl.ds(p * half + k * size, size)],
            keep_sem.at[k],
        )

    def finish(k):
        give_back(k).start()
        keep(k).start()

    def chunk_pieces(k):
        return [i for i, (lo, hi) in enumerate(pieces) if b0[k] <= lo and hi <= b0[k + 1]]

    ahead = 2
    lead = min(4, chunks)
    for k in range(min(ahead, chunks)):
        for i in chunk_pieces(k):
            swap(i).start()
    for i in range(len(pieces)):
        own(i).start()
    raw_copy = pltpu.make_async_copy(raw, plain, raw_sem)

    @pl.when(is_source)
    def _():
        raw_copy.start()

    @pl.when(q == 0)
    def _():
        for zh in (zh1, zh2):
            zh[0] = jnp.zeros_like(zh[0])

    @pl.when(q == nq - 1)
    def _():
        for zh in (zh1, zh2):
            zh[1] = jnp.zeros_like(zh[1])

    for i in range(len(pieces)):
        own(i).wait()
    for k in range(lead):
        for copy in edge(f0, xh1, x1_s, x1_r, p, k, 0, b1):
            copy.start()

    @pl.when(is_source)
    def _():
        raw_copy.wait()
        kern[...] = jnp.zeros_like(kern)
        gap = jnp.zeros((WIDE - BASIS_SIZE, BASIS_SIZE), jnp.float32)

        def widen(g, carry):
            lo = pl.multiple_of(g * (2 * BASIS_SIZE), 2 * BASIS_SIZE)
            both = plain[pl.ds(lo, 2 * BASIS_SIZE), :].astype(jnp.float32)
            both = jnp.concatenate([both[:BASIS_SIZE], gap, both[BASIS_SIZE:], gap], axis=0)
            hi = pl.multiple_of(g * (2 * WIDE), 2 * WIDE)
            kern[pl.ds(hi, 2 * WIDE), 0:BASIS_SIZE] = both.astype(jnp.bfloat16)
            return carry

        lax.fori_loop(0, BASIS_SIZE // 2, widen, 0)

    for t in range(chunks + 7):
        if t < chunks:
            for i in chunk_pieces(t):
                swap_in(i).wait_recv()
            if t + ahead < chunks:
                for i in chunk_pieces(t + ahead):
                    swap(i).start()
            for copy in edge(f0, xh1, x1_s, x1_r, other, t, 1, b1):
                copy.start()
            if t + lead < chunks:
                for copy in edge(f0, xh1, x1_s, x1_r, p, t + lead, 0, b1):
                    copy.start()
        if 0 <= t - 1 < chunks:
            i = t - 1
            for slot, blk in enumerate((p, other)):
                for copy in edge(f0, xh1, x1_s, x1_r, blk, i, slot, b1):
                    copy.wait_recv()
            slopes(f0, xh1, de1, b1[i], b1[i + 1])
            z_start(de1, zh1, z1_s, z1_r, i, b1)
        if 0 <= t - 2 < chunks:
            i = t - 2
            z_arrived(de1, zh1, z1_s, z1_r, i, b1)
            substep(f0, xh1, zh1, f1, b1[i], b1[i + 1])
            for blk in range(2):
                for copy in edge(f1, xh2, x2_s, x2_r, blk, i, blk, b2):
                    copy.start()
        if 0 <= t - 3 < chunks:
            i = t - 3
            for blk in range(2):
                for copy in edge(f1, xh2, x2_s, x2_r, blk, i, blk, b2):
                    copy.wait_recv()
            slopes(f1, xh2, de2, b2[i], b2[i + 1])
            z_start(de2, zh2, z2_s, z2_r, i, b2)
        if 0 <= t - 4 < chunks:
            i = t - 4
            z_arrived(de2, zh2, z2_s, z2_r, i, b2)
            substep(f1, xh2, zh2, tr, b2[i], b2[i + 1])

            @pl.when(is_source)
            def _(i=i):
                take_low(i)
                for d in range(1, ns):
                    low_copy(i, d).start()

            @pl.when(jnp.logical_not(is_source))
            def _(i=i):
                finish(i)

        @pl.when(is_source)
        def _(t=t):
            if 0 <= t - 5 < chunks:
                i = t - 5
                for d in range(1, ns):
                    low_copy(i, d).wait_recv()
                collide(i)
                for d in range(1, ns):
                    rate_copy(i, d).start()
                lift(i, rx[i], q)
            if 0 <= t - 6 < chunks:
                i = t - 6
                for d in range(1, ns):
                    rate_copy(i, d).wait_recv()
                    lift(i, rr[i, d - 1], lax.rem(q + ns - d, ns))
                finish(i)

    for k in range(chunks):
        z_sent(de1, zh1, z1_s, z1_r, k, b1)
        z_sent(de2, zh2, z2_s, z2_r, k, b2)
        for slot, blk in enumerate((p, other)):
            for copy in edge(f0, xh1, x1_s, x1_r, blk, k, slot, b1):
                copy.wait_send()
        for blk in range(2):
            for copy in edge(f1, xh2, x2_s, x2_r, blk, k, blk, b2):
                copy.wait_send()
    for i in range(len(pieces)):
        swap(i).wait_send()

    @pl.when(is_source)
    def _():
        for k in range(chunks):
            for d in range(1, ns):
                low_copy(k, d).wait_send()
                rate_copy(k, d).wait_send()

    for k in range(chunks):
        keep(k).wait()
        give_back(k).wait_send()
        got_back(k).wait_recv()


def body(hermite_coefficient_array, encounter_kernel_array, obstacle_indicator):
    planes, rows_y, rows_z, local = hermite_coefficient_array.shape
    nc = lax.axis_size("cells")
    nm = lax.axis_size("modes")
    per = local // BLOCK
    levels = 2 * per
    half = rows_y // 2
    ns = -(-(LDEG + 1) // levels)
    chunks = 8
    size = half // chunks
    part = size // ns
    ext = half + 4
    m = lax.axis_index("modes")
    first_a = (m // 2) * levels

    gas = jnp.where(obstacle_indicator != 0, 0.0, CFL).astype(jnp.float32)
    gas = jnp.concatenate([gas[:, -2:], gas, gas[:, :2]], axis=1)
    gas = lax.dynamic_slice_in_dim(gas, (m % 2) * half, ext, axis=1)
    mask = jnp.broadcast_to(gas[..., None], (planes, ext, rows_z, BLOCK))

    lane = jnp.arange(BLOCK, dtype=jnp.int32)
    lane_b, lane_c = lane // MC, lane % MC
    level = first_a + jnp.arange(levels, dtype=jnp.int32)[:, None] + 0 * lane[None, :]

    def down(x):
        return jnp.sqrt(x.astype(jnp.float32))

    def up(x, count):
        return jnp.where(x + 1 < count, jnp.sqrt((x + 1).astype(jnp.float32)), 0.0)

    coef = -0.5 * jnp.concatenate(
        [
            jnp.stack([down(lane_b), up(lane_b, MB), down(lane_c), up(lane_c, MC)]),
            down(level),
            up(level, MA),
            jnp.zeros(((-(4 + 2 * levels)) % 8, BLOCK), jnp.float32),
        ],
        axis=0,
    )

    index = np.arange(MODES)
    flags = (index // BLOCK + index // MC % MB + index % MC <= LDEG).astype(np.int32)
    rank = jnp.asarray(np.where(flags == 1, np.cumsum(flags) - 1, -1), jnp.int32)
    mine = lax.dynamic_slice_in_dim(rank, first_a * BLOCK, levels * BLOCK).reshape(levels, BLOCK)
    wide = jnp.arange(WIDE, dtype=jnp.int32)
    sel = (mine[:, :, None] == wide[None, None, :]).astype(jnp.bfloat16)
    sel_t = (mine[:, None, :] == wide[None, :, None]).astype(jnp.bfloat16)

    b2 = [2 + size * k for k in range(chunks + 1)]
    count = len(pieces_of([0] + [b + 2 for b in b2[1:]], half))
    peers = max(ns - 1, 1)
    cells = planes * part * rows_z
    field = pltpu.VMEM((2, planes, ext, rows_z, local), jnp.float32)
    halo = pltpu.VMEM((2, 2, ext, rows_z, local), jnp.float32)
    slope = pltpu.VMEM((2, planes, ext, rows_z, BLOCK), jnp.float32)
    dma = pltpu.SemaphoreType.DMA
    cfg = (planes, rows_y, rows_z, local, nc, nm, ns, chunks)
    vmem = pl.BlockSpec(memory_space=pltpu.VMEM)
    return pl.pallas_call(
        functools.partial(kernel, cfg),
        out_shape=jax.ShapeDtypeStruct(hermite_coefficient_array.shape, jnp.float32),
        in_specs=[pl.BlockSpec(memory_space=pl.ANY)] + [vmem] * 4 + [pl.BlockSpec(memory_space=pl.ANY)],
        out_specs=pl.BlockSpec(memory_space=pl.ANY),
        scratch_shapes=[
            field, field, field, halo, halo, slope, slope, slope, slope,
            pltpu.VMEM((chunks, ns, cells, WIDE), jnp.float32),
            pltpu.VMEM((chunks, peers, cells, WIDE), jnp.float32),
            pltpu.VMEM((chunks, cells, WIDE), jnp.float32),
            pltpu.VMEM((chunks, peers, cells, WIDE), jnp.float32),
            pltpu.VMEM((BASIS_SIZE * BASIS_SIZE, BASIS_SIZE), jnp.bfloat16),
            pltpu.VMEM((BASIS_SIZE * WIDE, WIDE), jnp.bfloat16),
            dma, dma((count,)), dma((count,)), dma((count,)),
            dma((2, 2, chunks)), dma((2, 2, chunks)), dma((2, 2, chunks)), dma((2, 2, chunks)),
            dma((2, chunks)), dma((2, chunks)), dma((2, chunks)), dma((2, chunks)),
            dma((chunks, peers)), dma((chunks, peers)), dma((chunks, peers)), dma((chunks, peers)),
            dma((chunks,)), dma((chunks,)), dma((chunks,)),
        ],
        compiler_params=pltpu.CompilerParams(
            collective_id=0, has_side_effects=True, vmem_limit_bytes=60 * 1024 * 1024
        ),
    )(hermite_coefficient_array, mask, coef, sel, sel_t, encounter_kernel_array)


def solution(mesh):
    placed = (P("cells", None, None, "modes"), P(), P("cells", None, None))
    return jax.shard_map(
        body, mesh=mesh, in_specs=placed, out_specs=P("cells", None, None, "modes"), check_vma=False
    )
```

```python
import functools
import math

import jax
import jax.numpy as jnp
import numpy as np
from jax import lax
from jax.experimental import pallas as pl
from jax.experimental.pallas import tpu as pltpu
from jax.sharding import PartitionSpec as P

MA = 16
MB = 16
MC = 8
LDEG = 7
BASIS_SIZE = 120
MODES = 2048
BLOCK = MB * MC
WIDE = 128
GROUP = 16

CFL = 0.04
DTC = 0.2
MESH = pl.DeviceIdType.MESH


def pieces_of(edges, half):
    marks = sorted(set(edges) | {2, half + 2})
    return [(lo, hi) for lo, hi in zip(marks[:-1], marks[1:])]


def split3(x):
    hi = x.astype(jnp.bfloat16)
    rest = x - hi.astype(jnp.float32)
    mid = rest.astype(jnp.bfloat16)
    low = (rest - mid.astype(jnp.float32)).astype(jnp.bfloat16)
    return hi, mid, low


def dot(a, b):
    return jnp.dot(a, b, preferred_element_type=jnp.float32)


def kernel(cfg, hin, mask, coef, sel, sel_t, raw, out, f0, f1, tr, xh1, xh2, zh1, zh2, de1, de2,
           lx, lr, rx, rr, table, lt, rt, raw_sem, loc_sem, swap_s, swap_r, x1_s, x1_r, x2_s, x2_r, z1_s, z1_r, z2_s, z2_r,
           low_s, low_r, rate_s, rate_r, back_s, back_r, keep_sem):
    planes, rows_y, rows_z, local, nc, nm, ns, chunks = cfg
    per = local // BLOCK
    levels = 2 * per
    half = rows_y // 2
    nq = nm // 2
    size = half // chunks
    b2 = [2 + size * k for k in range(chunks + 1)]
    b1 = [1] + [b + 1 for b in b2[1:]]
    b0 = [0] + [b + 2 for b in b2[1:]]
    part = size // ns

    c = lax.axis_index("cells")
    m = lax.axis_index("modes")
    p = lax.rem(m, 2)
    q = lax.div(m, 2)
    other = 1 - p
    mate = (c, q * 2 + other)
    before = (lax.rem(c + nc - 1, nc), m)
    after = (lax.rem(c + 1, nc), m)
    below = (c, m - 2)
    above = (c, m + 2)
    has_below = q > 0
    has_above = q < nq - 1
    is_source = q < ns

    def peer(d):
        return (c, lax.rem(q + d, ns) * 2 + p)

    barrier = pltpu.get_barrier_semaphore()

    def greet(dev):
        pl.semaphore_signal(barrier, inc=1, device_id=dev, device_id_type=MESH)

    for dev in (mate, before, after):
        greet(dev)

    @pl.when(has_below)
    def _():
        greet(below)

    @pl.when(has_above)
    def _():
        greet(above)

    @pl.when(is_source)
    def _():
        for d in range(1, ns):
            greet(peer(d))

    greeted = 3 + has_below.astype(jnp.int32) + has_above.astype(jnp.int32)
    pl.semaphore_wait(barrier, greeted + (ns - 1) * is_source.astype(jnp.int32))

    def remote(src, dst, s, r, dev):
        return pltpu.make_async_remote_copy(
            src_ref=src, dst_ref=dst, send_sem=s, recv_sem=r, device_id=dev, device_id_type=MESH
        )

    pieces = pieces_of(b0, half)

    def grid_row(side, e):
        return lax.rem(side * half + (rows_y - 2) + e, rows_y)

    def swap(i):
        lo, hi = pieces[i]
        return remote(
            hin.at[:, pl.ds(grid_row(other, lo), hi - lo)],
            f0.at[p, :, pl.ds(lo, hi - lo)],
            swap_s.at[i], swap_r.at[i], mate,
        )

    def swap_in(i):
        lo, hi = pieces[i]
        return remote(
            hin.at[:, pl.ds(grid_row(other, lo), hi - lo)],
            f0.at[other, :, pl.ds(lo, hi - lo)],
            swap_s.at[i], swap_r.at[i], mate,
        )

    def own(i):
        lo, hi = pieces[i]
        return pltpu.make_async_copy(
            hin.at[:, pl.ds(grid_row(p, lo), hi - lo)],
            f0.at[p, :, pl.ds(lo, hi - lo)],
            loc_sem.at[i],
        )

    def edge(field, halo, ss, rs, blk, k, slot, bounds):
        n = bounds[k + 1] - bounds[k]
        where = pl.ds(bounds[k], n)
        up = remote(field.at[blk, planes - 1, where], halo.at[0, blk, where],
                    ss.at[0, slot, k], rs.at[0, slot, k], after)
        down = remote(field.at[blk, 0, where], halo.at[1, blk, where],
                      ss.at[1, slot, k], rs.at[1, slot, k], before)
        return up, down

    def lanes(j):
        return pl.ds((j % per) * BLOCK, BLOCK)

    def gradient(field, halo, pln, e, j):
        blk = j // per
        nxt = halo[1, blk, e, :, lanes(j)] if pln == planes - 1 else field[blk, pln + 1, e, :, lanes(j)]
        prv = halo[0, blk, e, :, lanes(j)] if pln == 0 else field[blk, pln - 1, e, :, lanes(j)]
        return nxt, prv

    def slopes(field, halo, de, lo, hi):
        def row(e, carry):
            for pln in range(planes):
                nxt, prv = gradient(field, halo, pln, e, 0)
                de[0, pln, e] = nxt - prv
                nxt, prv = gradient(field, halo, pln, e, levels - 1)
                de[1, pln, e] = nxt - prv
            return carry

        lax.fori_loop(lo, hi, row, 0)

    def to_below(de, zh, ss, rs, k, bounds):
        where = pl.ds(bounds[k], bounds[k + 1] - bounds[k])
        return remote(de.at[0, :, where], zh.at[1, :, where], ss.at[0, k], rs.at[0, k], below)

    def to_above(de, zh, ss, rs, k, bounds):
        where = pl.ds(bounds[k], bounds[k + 1] - bounds[k])
        return remote(de.at[1, :, where], zh.at[0, :, where], ss.at[1, k], rs.at[1, k], above)

    def z_start(*a):
        @pl.when(has_below)
        def _():
            to_below(*a).start()

        @pl.when(has_above)
        def _():
            to_above(*a).start()

    def z_arrived(*a):
        @pl.when(has_below)
        def _():
            to_above(*a).wait_recv()

        @pl.when(has_above)
        def _():
            to_below(*a).wait_recv()

    def z_sent(*a):
        @pl.when(has_below)
        def _():
            to_below(*a).wait_send()

        @pl.when(has_above)
        def _():
            to_above(*a).wait_send()

    wx = 0.5 * 2.0 * math.sqrt(MA)
    wy = 0.5 * 2.0 * math.sqrt(MB)
    wz = 0.5 * 2.0 * math.sqrt(MC)
    wc = 2.0 * (wx + wy + wz)

    def substep(field, halo, zh, dest, lo, hi):
        def row(e, carry):
            for pln in range(planes):
                gas = mask[pln, e]
                pairs = [gradient(field, halo, pln, e, j) for j in range(levels)]
                grads = [zh[0, pln, e]] + [a - b for a, b in pairs] + [zh[1, pln, e]]
                for j in range(levels):
                    blk = j // per
                    mid = field[blk, pln, e, :, lanes(j)]
                    ny = field[blk, pln, e + 1, :, lanes(j)]
                    py = field[blk, pln, e - 1, :, lanes(j)]
                    nz = pltpu.roll(mid, rows_z - 1, 0)
                    pz = pltpu.roll(mid, 1, 0)
                    dy = ny - py
                    dz = nz - pz
                    acc = coef[4 + j : 5 + j, :] * grads[j]
                    acc += coef[4 + levels + j : 5 + levels + j, :] * grads[j + 2]
                    acc += coef[0:1, :] * pltpu.roll(dy, MC, 1)
                    acc += coef[1:2, :] * pltpu.roll(dy, BLOCK - MC, 1)
                    acc += coef[2:3, :] * pltpu.roll(dz, 1, 1)
                    acc += coef[3:4, :] * pltpu.roll(dz, BLOCK - 1, 1)
                    acc += wx * (pairs[j][0] + pairs[j][1]) + wy * (ny + py) + wz * (nz + pz) - wc * mid
                    dest[blk, pln, e, :, lanes(j)] = mid + gas * acc
            return carry

        lax.fori_loop(lo, hi, row, 0)

    def take_low(k):
        for t in range(ns):
            lo = b2[k] + t * part
            for pln in range(planes):
                total = jnp.zeros((part * rows_z, WIDE), jnp.float32)
                for j in range(levels):
                    x = tr[j // per, pln, lo : lo + part, :, lanes(j)].reshape(part * rows_z, BLOCK)
                    for term in split3(x):
                        total += dot(term, sel[j])
                lx[k, t, pln * part * rows_z : (pln + 1) * part * rows_z] = total

    def low_copy(k, d):
        return remote(lx.at[k, lax.rem(q + d, ns)], lr.at[k, d - 1],
                      low_s.at[k, d - 1], low_r.at[k, d - 1], peer(d))

    def rate_copy(k, d):
        return remote(rx.at[k], rr.at[k, d - 1], rate_s.at[k, d - 1], rate_r.at[k, d - 1], peer(d))

    def collide(k):
        low = lx[k, q]
        for d in range(1, ns):
            low = low + lr[k, d - 1]
        lt[...] = low.T
        rt[...] = jnp.zeros_like(rt)

        def step(first, count, columns):
            rows = lt[pl.ds(first, count), :]
            values = lt[0:BASIS_SIZE, :]
            factors = jnp.concatenate(
                [(rows[i : i + 1, :] * values) for i in range(count)], axis=0
            ).astype(jnp.bfloat16)
            rt[0:BASIS_SIZE, :] += dot(table[:, columns], factors)

        def whole(g, carry):
            width = GROUP * BASIS_SIZE
            step(pl.multiple_of(g * GROUP, GROUP), GROUP, pl.ds(pl.multiple_of(g * width, WIDE), width))
            return carry

        groups = BASIS_SIZE // GROUP
        lax.fori_loop(0, groups, whole, 0)
        if groups * GROUP < BASIS_SIZE:
            step(groups * GROUP, BASIS_SIZE - groups * GROUP,
                 pl.ds(groups * GROUP * BASIS_SIZE, (BASIS_SIZE - groups * GROUP) * BASIS_SIZE))
        rx[k] = rt[...].T

    def lift(k, rates, t):
        lo = b2[k] + t * part
        terms = split3(rates)
        for j in range(levels):
            add = sum(dot(term, sel_t[j]) for term in terms) * DTC
            for pln in range(planes):
                one = add[pln * part * rows_z : (pln + 1) * part * rows_z]
                tr[j // per, pln, pl.ds(lo, part), :, lanes(j)] += one.reshape(part, rows_z, BLOCK)

    def give_back(k):
        return remote(
            tr.at[other, :, pl.ds(b2[k], size)],
            out.at[:, pl.ds(p * half + k * size, size)],
            back_s.at[k], back_r.at[k], mate,
        )

    def got_back(k):
        return remote(
            tr.at[other, :, pl.ds(b2[k], size)],
            out.at[:, pl.ds(other * half + k * size, size)],
            back_s.at[k], back_r.at[k], mate,
        )

    def keep(k):
        return pltpu.make_async_copy(
            tr.at[p, :, pl.ds(b2[k], size)],
            out.at[:, pl.ds(p * half + k * size, size)],
            keep_sem.at[k],
        )

    def finish(k):
        give_back(k).start()
        keep(k).start()

    def chunk_pieces(k):
        return [i for i, (lo, hi) in enumerate(pieces) if b0[k] <= lo and hi <= b0[k + 1]]

    ahead = 2
    lead = min(4, chunks)
    for k in range(min(ahead, chunks)):
        for i in chunk_pieces(k):
            swap(i).start()
    for i in range(len(pieces)):
        own(i).start()
    raw_copy = pltpu.make_async_copy(raw, table, raw_sem)

    @pl.when(is_source)
    def _():
        raw_copy.start()

    @pl.when(q == 0)
    def _():
        for zh in (zh1, zh2):
            zh[0] = jnp.zeros_like(zh[0])

    @pl.when(q == nq - 1)
    def _():
        for zh in (zh1, zh2):
            zh[1] = jnp.zeros_like(zh[1])

    for i in range(len(pieces)):
        own(i).wait()
    for k in range(lead):
        for copy in edge(f0, xh1, x1_s, x1_r, p, k, 0, b1):
            copy.start()

    @pl.when(is_source)
    def _():
        raw_copy.wait()

    for t in range(chunks + 7):
        if t < chunks:
            for i in chunk_pieces(t):
                swap_in(i).wait_recv()
            if t + ahead < chunks:
                for i in chunk_pieces(t + ahead):
                    swap(i).start()
            for copy in edge(f0, xh1, x1_s, x1_r, other, t, 1, b1):
                copy.start()
            if t + lead < chunks:
                for copy in edge(f0, xh1, x1_s, x1_r, p, t + lead, 0, b1):
                    copy.start()
        if 0 <= t - 1 < chunks:
            i = t - 1
            for slot, blk in enumerate((p, other)):
                for copy in edge(f0, xh1, x1_s, x1_r, blk, i, slot, b1):
                    copy.wait_recv()
            slopes(f0, xh1, de1, b1[i], b1[i + 1])
            z_start(de1, zh1, z1_s, z1_r, i, b1)
        if 0 <= t - 2 < chunks:
            i = t - 2
            z_arrived(de1, zh1, z1_s, z1_r, i, b1)
            substep(f0, xh1, zh1, f1, b1[i], b1[i + 1])
            for blk in range(2):
                for copy in edge(f1, xh2, x2_s, x2_r, blk, i, blk, b2):
                    copy.start()
        if 0 <= t - 3 < chunks:
            i = t - 3
            for blk in range(2):
                for copy in edge(f1, xh2, x2_s, x2_r, blk, i, blk, b2):
                    copy.wait_recv()
            slopes(f1, xh2, de2, b2[i], b2[i + 1])
            z_start(de2, zh2, z2_s, z2_r, i, b2)
        if 0 <= t - 4 < chunks:
            i = t - 4
            z_arrived(de2, zh2, z2_s, z2_r, i, b2)
            substep(f1, xh2, zh2, tr, b2[i], b2[i + 1])

            @pl.when(is_source)
            def _(i=i):
                take_low(i)
                for d in range(1, ns):
                    low_copy(i, d).start()

            @pl.when(jnp.logical_not(is_source))
            def _(i=i):
                finish(i)

        @pl.when(is_source)
        def _(t=t):
            if 0 <= t - 5 < chunks:
                i = t - 5
                for d in range(1, ns):
                    low_copy(i, d).wait_recv()
                collide(i)
                for d in range(1, ns):
                    rate_copy(i, d).start()
                lift(i, rx[i], q)
            if 0 <= t - 6 < chunks:
                i = t - 6
                for d in range(1, ns):
                    rate_copy(i, d).wait_recv()
                    lift(i, rr[i, d - 1], lax.rem(q + ns - d, ns))
                finish(i)

    for k in range(chunks):
        z_sent(de1, zh1, z1_s, z1_r, k, b1)
        z_sent(de2, zh2, z2_s, z2_r, k, b2)
        for slot, blk in enumerate((p, other)):
            for copy in edge(f0, xh1, x1_s, x1_r, blk, k, slot, b1):
                copy.wait_send()
        for blk in range(2):
            for copy in edge(f1, xh2, x2_s, x2_r, blk, k, blk, b2):
                copy.wait_send()
    for i in range(len(pieces)):
        swap(i).wait_send()

    @pl.when(is_source)
    def _():
        for k in range(chunks):
            for d in range(1, ns):
                low_copy(k, d).wait_send()
                rate_copy(k, d).wait_send()

    for k in range(chunks):
        keep(k).wait()
        give_back(k).wait_send()
        got_back(k).wait_recv()


def body(hermite_coefficient_array, encounter_kernel_array, obstacle_indicator):
    planes, rows_y, rows_z, local = hermite_coefficient_array.shape
    nc = lax.axis_size("cells")
    nm = lax.axis_size("modes")
    per = local // BLOCK
    levels = 2 * per
    half = rows_y // 2
    ns = -(-(LDEG + 1) // levels)
    chunks = 8
    size = half // chunks
    part = size // ns
    ext = half + 4
    m = lax.axis_index("modes")
    first_a = (m // 2) * levels

    gas = jnp.where(obstacle_indicator != 0, 0.0, CFL).astype(jnp.float32)
    gas = jnp.concatenate([gas[:, -2:], gas, gas[:, :2]], axis=1)
    gas = lax.dynamic_slice_in_dim(gas, (m % 2) * half, ext, axis=1)
    mask = jnp.broadcast_to(gas[..., None], (planes, ext, rows_z, BLOCK))

    lane = jnp.arange(BLOCK, dtype=jnp.int32)
    lane_b, lane_c = lane // MC, lane % MC
    level = first_a + jnp.arange(levels, dtype=jnp.int32)[:, None] + 0 * lane[None, :]

    def down(x):
        return jnp.sqrt(x.astype(jnp.float32))

    def up(x, count):
        return jnp.where(x + 1 < count, jnp.sqrt((x + 1).astype(jnp.float32)), 0.0)

    coef = -0.5 * jnp.concatenate(
        [
            jnp.stack([down(lane_b), up(lane_b, MB), down(lane_c), up(lane_c, MC)]),
            down(level),
            up(level, MA),
            jnp.zeros(((-(4 + 2 * levels)) % 8, BLOCK), jnp.float32),
        ],
        axis=0,
    )

    index = np.arange(MODES)
    flags = (index // BLOCK + index // MC % MB + index % MC <= LDEG).astype(np.int32)
    rank = jnp.asarray(np.where(flags == 1, np.cumsum(flags) - 1, -1), jnp.int32)
    mine = lax.dynamic_slice_in_dim(rank, first_a * BLOCK, levels * BLOCK).reshape(levels, BLOCK)
    wide = jnp.arange(WIDE, dtype=jnp.int32)
    sel = (mine[:, :, None] == wide[None, None, :]).astype(jnp.bfloat16)
    sel_t = (mine[:, None, :] == wide[None, :, None]).astype(jnp.bfloat16)

    b2 = [2 + size * k for k in range(chunks + 1)]
    count = len(pieces_of([0] + [b + 2 for b in b2[1:]], half))
    peers = max(ns - 1, 1)
    cells = planes * part * rows_z
    field = pltpu.VMEM((2, planes, ext, rows_z, local), jnp.float32)
    halo = pltpu.VMEM((2, 2, ext, rows_z, local), jnp.float32)
    slope = pltpu.VMEM((2, planes, ext, rows_z, BLOCK), jnp.float32)
    dma = pltpu.SemaphoreType.DMA
    cfg = (planes, rows_y, rows_z, local, nc, nm, ns, chunks)
    vmem = pl.BlockSpec(memory_space=pltpu.VMEM)
    return pl.pallas_call(
        functools.partial(kernel, cfg),
        out_shape=jax.ShapeDtypeStruct(hermite_coefficient_array.shape, jnp.float32),
        in_specs=[pl.BlockSpec(memory_space=pl.ANY)] + [vmem] * 4 + [pl.BlockSpec(memory_space=pl.ANY)],
        out_specs=pl.BlockSpec(memory_space=pl.ANY),
        scratch_shapes=[
            field, field, field, halo, halo, slope, slope, slope, slope,
            pltpu.VMEM((chunks, ns, cells, WIDE), jnp.float32),
            pltpu.VMEM((chunks, peers, cells, WIDE), jnp.float32),
            pltpu.VMEM((chunks, cells, WIDE), jnp.float32),
            pltpu.VMEM((chunks, peers, cells, WIDE), jnp.float32),
            pltpu.VMEM((BASIS_SIZE, BASIS_SIZE * BASIS_SIZE), jnp.bfloat16),
            pltpu.VMEM((WIDE, cells), jnp.float32),
            pltpu.VMEM((WIDE, cells), jnp.float32),
            dma, dma((count,)), dma((count,)), dma((count,)),
            dma((2, 2, chunks)), dma((2, 2, chunks)), dma((2, 2, chunks)), dma((2, 2, chunks)),
            dma((2, chunks)), dma((2, chunks)), dma((2, chunks)), dma((2, chunks)),
            dma((chunks, peers)), dma((chunks, peers)), dma((chunks, peers)), dma((chunks, peers)),
            dma((chunks,)), dma((chunks,)), dma((chunks,)),
        ],
        compiler_params=pltpu.CompilerParams(
            collective_id=0, has_side_effects=True, vmem_limit_bytes=60 * 1024 * 1024
        ),
    )(hermite_coefficient_array, mask, coef, sel, sel_t, encounter_kernel_array.T)


def solution(mesh):
    placed = (P("cells", None, None, "modes"), P(), P("cells", None, None))
    return jax.shard_map(
        body, mesh=mesh, in_specs=placed, out_specs=P("cells", None, None, "modes"), check_vma=False
    )
```
